32 devices in a mesh: rows: 8 (over z, y), code: 4 (over x, core).
Axes of the slice: x: 2, y: 2, z: 4, core: 2. Of those that a mesh axis runs over, the one named last changes fastest.
Arguments:
- embedding_vectors: bfloat16 [3072, 256], P('rows'), may hold values from -45.3125 to 45.3125
- codebook: bfloat16 [65536, 256], P(('code', 'rows')), may hold values from -0.38125 to 0.38125
- weights: float32 [3072], P('rows'), may hold values from 0.6 to 4.2
Outputs:
- gradient: float32 [65536, 256], P(('code', 'rows'))
- load: float32 [65536], P(('code', 'rows'))
The draws below stay inside these ranges and needn't reach their ends.
All inputs are finite; a program needn't handle non-finite values.
Results may differ from the reference program's by a relative error of at most 0.013.
Values may be sent and summed in bfloat16 or wider, within the bound.
No kernel may reach another device: no remote copies, remote signals or barrier semaphores. Data moves between devices by JAX's collectives and lax.ppermute only.
A program may use at most 128 MiB of HBM per device.

```python
import jax
import jax.numpy as jnp
from jax import lax

D = 256
K = 65536
ITERS = 3
ROWS = 3072


def codebook_base(key):
    scale_factor = D ** (-0.5)
    base = jnp.clip(jax.random.normal(jax.random.fold_in(key, 11), (K, D), jnp.float32), -6.0, 6.0) * scale_factor
    return base


def draw_codebook(key, part):
    return codebook_base(key).astype(jnp.bfloat16)


def draw_embedding_vectors(key, part):
    row_scales = jnp.exp(jax.random.uniform(jax.random.fold_in(key, 12), (ROWS,), jnp.float32, jnp.log(0.3), jnp.log(3.0)))
    values = jnp.clip(jax.random.normal(jax.random.fold_in(key, 13), (ROWS, D), jnp.float32), -6.0, 6.0)
    result = values * row_scales[:, None]
    return result.astype(jnp.bfloat16)


def draw_weights(key, part):
    index = jnp.arange(ROWS).astype(jnp.float32)
    ramp = 1.0 + 2.0 * index / (ROWS - 1)
    factor = jax.random.uniform(jax.random.fold_in(key, 21), (ROWS,), jnp.float32, 0.6, 1.4)
    return ramp * factor


def setup_inputs(seed: int = 0) -> dict:
    keys = jax.random.split(jax.random.key(seed), 4)
    return {
        "embedding_vectors": draw_embedding_vectors(jax.random.fold_in(keys[3], 71), 0),
        "codebook": draw_codebook(jax.random.fold_in(keys[3], 71), 0),
        "weights": draw_weights(jax.random.fold_in(keys[3], 71), 0),
    }


sharpness_factor = 2.0


def reference(embedding_vectors, codebook, weights):
    block_size = min(K, 4096)
    block_list = K // block_size
    stacked = codebook.reshape(block_list, block_size, D)
    balance = ROWS / K

    def scores_of(centroid_slab):
        return sharpness_factor * jnp.dot(embedding_vectors, centroid_slab.T, preferred_element_type=jnp.float32)

    def maximum_step(carry, centroid_slab):
        return jnp.maximum(carry, jnp.max(scores_of(centroid_slab), axis=1)), None

    row_peak, unused = lax.scan(maximum_step, jnp.full((ROWS,), -jnp.inf, jnp.float32), stacked)

    def exponent_of(centroid_slab):
        return jnp.exp(scores_of(centroid_slab) - row_peak[:, None])

    def marginal_per_sample(col_scale):
        def increment_update(carry, pair):
            centroid_slab, scale_block = pair
            return carry + jnp.dot(exponent_of(centroid_slab), scale_block, precision=lax.Precision.HIGHEST), None
        total_sums, discarded_output = lax.scan(increment_update, jnp.zeros((ROWS,), jnp.float32), (stacked, col_scale.reshape(block_list, block_size)))
        return total_sums

    def column_totals(row_scale):
        def one_block(centroid_slab):
            return jnp.dot(row_scale, exponent_of(centroid_slab), precision=lax.Precision.HIGHEST)
        return lax.map(one_block, stacked).reshape(K)

    col_scale = jnp.ones((K,), jnp.float32)
    row_scale = weights / marginal_per_sample(col_scale)
    for iteration in range(ITERS):
        col_scale = balance / column_totals(row_scale)
        row_scale = weights / marginal_per_sample(col_scale)

    def final_block(pair):
        centroid_slab, scale_block = pair
        transport_plan = exponent_of(centroid_slab) * row_scale[:, None] * scale_block[None, :]
        block_mass = jnp.sum(transport_plan, axis=0)
        block_sums = jnp.dot(transport_plan.astype(jnp.bfloat16).T, embedding_vectors, preferred_element_type=jnp.float32)
        return block_sums, block_mass

    codeword_sums, code_mass = lax.map(final_block, (stacked, col_scale.reshape(block_list, block_size)))
    codeword_sums = codeword_sums.reshape(K, D)
    code_mass = code_mass.reshape(K)
    gradient = (code_mass[:, None] * codebook.astype(jnp.float32) - codeword_sums) / balance
    return gradient, code_mass / balance
```

```python
import functools

import jax
import jax.numpy as jnp
from jax import lax
from jax.experimental import pallas as pl
from jax.experimental.pallas import tpu as pltpu
from jax.sharding import PartitionSpec as P

ITERS = 3
SHARP = 2.0
LOG2E = 1.4426950408889634
AXES = ("rows", "code")
LANES = 128
VMEM_LIMIT = 60 * 1024 * 1024
NT = (((1,), (1,)), ((), ()))
NN = (((1,), (0,)), ((), ()))


def bit_groups(size):
    bits = [1 << b for b in range(size.bit_length() - 1)][::-1]
    return [tuple(bits[i : i + 2]) for i in range(0, len(bits), 2)]


def exchange(x, mask, size):
    return lax.ppermute(x, AXES, [(i, i ^ mask) for i in range(size)])


def gather_pieces(piece, size):
    out = piece[None]
    for group in bit_groups(size):
        masks = group if len(group) == 1 else (group[1], group[0], group[0] ^ group[1])
        out = jnp.concatenate([out] + [exchange(out, m, size) for m in masks], axis=0)
    return out


def slot_of(distance, size):
    slot, place = 0, 1
    for group in bit_groups(size):
        for bit in group[::-1]:
            slot = slot + jnp.where((distance & bit) != 0, place, 0)
            place *= 2
    return slot


def split2(x):
    hi = x.astype(jnp.bfloat16)
    lo = (x - hi.astype(jnp.float32)).astype(jnp.bfloat16)
    return hi, lo


def load_block(me_ref, pieces_ref, block, size, code):
    me = me_ref[0]
    parts = []
    for c in range(code):
        parts.append(pieces_ref[slot_of(me ^ (block * code + c), size)])
    return jnp.concatenate(parts, axis=0)


def exponent_body(me_ref, pieces_ref, book_ref, x_ref, peak_ref, lse_ref, scores, *, size, code, kb):
    rows = load_block(me_ref, pieces_ref, pl.program_id(0), size, code)
    n = rows.shape[0]
    kl = book_ref.shape[0]
    peak = jnp.full((8, n), -jnp.inf, jnp.float32)
    for k in range(0, kl, kb):
        s = lax.dot_general(book_ref[k : k + kb, :], rows, NT, preferred_element_type=jnp.float32)
        scores[k : k + kb, :] = s
        peak = jnp.maximum(peak, jnp.max(s.reshape(kb // 8, 8, n), axis=0))
    peak = jnp.max(peak, axis=0, keepdims=True)
    scale = SHARP * LOG2E
    total = jnp.zeros((8, n), jnp.float32)
    for k in range(0, kl, kb):
        e = jnp.exp2((scores[k : k + kb, :] - peak) * scale)
        x_ref[k : k + kb, :] = e.astype(jnp.bfloat16)
        total = total + jnp.sum(e.reshape(kb // 8, 8, n), axis=0)
    total = jnp.sum(total, axis=0, keepdims=True)
    peak_ref[...] = (peak * SHARP)[None]
    lse_ref[...] = (peak * SHARP + jnp.log(total))[None]


def to_tiles(dst, row, n):
    for t in range(n // LANES):
        dst[t : t + 1, :] = row[:, t * LANES : (t + 1) * LANES]


def to_lanes(dst, tiles, n):
    for t in range(n // LANES):
        dst[:, t * LANES : (t + 1) * LANES] = jnp.broadcast_to(tiles[t : t + 1, :], (dst.shape[0], LANES))


def row_factor(first, got_ref, peak_ref, w_ref, factor_ref, nt):
    if first:
        got = got_ref[:, :nt, :]
        top = jnp.max(got, axis=0)
        common = top + jnp.log(jnp.sum(jnp.exp(got - top[None]), axis=0))
        factor = jnp.exp(peak_ref[...] - common)
        return w_ref[...] * factor, factor
    total = jnp.sum(got_ref[...].astype(jnp.float32), axis=0)
    factor = factor_ref[...]
    return w_ref[...] / total * factor, factor


def iterate_body(*refs, first, balance):
    if first:
        got_ref, peak_ref, w_ref, x_ref, col_ref, send_ref, factor_out, lhs, acc, fac = refs
        factor_ref = None
    else:
        got_ref, factor_ref, w_ref, x_ref, col_ref, send_ref, lhs, acc, fac = refs
        peak_ref = None
    nt = w_ref.shape[0]
    n = nt * LANES
    step = pl.program_id(0)

    @pl.when(step == 0)
    def _():
        r, factor = row_factor(first, got_ref, peak_ref, w_ref, factor_ref, nt)
        fac[...] = factor
        if first:
            factor_out[...] = factor
        put_rows(lhs, r, n)
        acc[...] = jnp.zeros(acc.shape, jnp.float32)

    x = x_ref[...]
    cols = lax.dot_general(lhs[...], x, NT, preferred_element_type=jnp.float32)
    col = balance / (cols[0:1] + cols[8:9])
    col_ref[...] = col
    hi, lo = split2(jnp.broadcast_to(col, (8, col.shape[1])))
    sums = lax.dot_general(jnp.concatenate([hi, lo], axis=0), x, NN, preferred_element_type=jnp.float32)
    acc[...] += sums[0:8] + sums[8:16]

    @pl.when(step == pl.num_programs(0) - 1)
    def _():
        for t in range(nt):
            part = acc[0:1, t * LANES : (t + 1) * LANES] * fac[t : t + 1, :]
            send_ref[:, t : t + 1, :] = jnp.broadcast_to(part.astype(jnp.bfloat16)[None], (send_ref.shape[0], 1, LANES))


def put_rows(lhs, r, n):
    hi, lo = split2(r)
    for t in range(n // LANES):
        lhs[0:8, t * LANES : (t + 1) * LANES] = jnp.broadcast_to(r[t : t + 1, :], (8, LANES)).astype(jnp.bfloat16)
        lhs[8:16, t * LANES : (t + 1) * LANES] = jnp.broadcast_to(
            r[t : t + 1, :] - hi[t : t + 1, :].astype(jnp.float32), (8, LANES)
        ).astype(jnp.bfloat16)


def final_body(me_ref, got_ref, factor_ref, w_ref, x_ref, col_ref, pieces_ref, book_ref, grad_ref, load_ref, lhs, weighted, *, size, code, rows, balance):
    nt = w_ref.shape[0]
    n = nt * LANES

    @pl.when(pl.program_id(0) == 0)
    def _():
        r, _ = row_factor(False, got_ref, None, w_ref, factor_ref, nt)
        put_rows(lhs, r, n)
        rt = r.T
        per = LANES
        for b in range(rows):
            block = load_block(me_ref, pieces_ref, b, size, code)
            for t in range(block.shape[0] // per):
                g = b * (block.shape[0] // per) + t
                scaled = block[t * per : (t + 1) * per, :].astype(jnp.float32) * rt[:, g : g + 1]
                weighted[g * per : (g + 1) * per, :] = scaled.astype(jnp.bfloat16)

    x = x_ref[...]
    cols = lax.dot_general(lhs[...], x, NT, preferred_element_type=jnp.float32)
    col = col_ref[...]
    mass = col * (cols[0:1] + cols[8:9]) / balance
    load_ref[...] = mass
    kb = x.shape[0]
    both = jnp.concatenate([mass, col / balance, jnp.zeros((6, kb), jnp.float32)], axis=0).T
    sums = jnp.dot(x, weighted[...], preferred_element_type=jnp.float32)
    grad_ref[...] = both[:, 0:1] * book_ref[...].astype(jnp.float32) - both[:, 1:2] * sums


def share_first(lse, weights, nt, rows, code):
    wt = weights.shape[0] // LANES
    size = rows * code
    if copies_of(size, nt) == 1:
        top = lax.pmax(lse, AXES)
        common = top + jnp.log(lax.psum(jnp.exp(lse - top), AXES))
        return common[None], lax.all_gather(weights, "rows", axis=0, tiled=True).reshape(nt, LANES)
    own = jnp.concatenate([lse, weights.reshape(wt, LANES)], axis=0)
    own = jnp.broadcast_to(own[None], (size, nt + wt, LANES))
    got = lax.all_to_all(own, AXES, split_axis=0, concat_axis=0, tiled=True)
    return got, got[::code, nt:, :].reshape(nt, LANES)


def share(send):
    if send.shape[0] == 1:
        return lax.psum(send.astype(jnp.float32), AXES)
    return lax.all_to_all(send, AXES, split_axis=0, concat_axis=0, tiled=True)


def copies_of(size, nt):
    return size if size * nt * LANES <= 1 << 20 else 1


def full(shape):
    return pl.BlockSpec(shape, lambda *_: (0,) * len(shape))


def local(embedding_vectors, codebook, weights):
    rows, code = lax.axis_size("rows"), lax.axis_size("code")
    size = rows * code
    shard, d = embedding_vectors.shape
    kl = codebook.shape[0]
    n = rows * shard
    nt = n // LANES
    balance = n / (size * kl)
    me = (lax.axis_index("rows") * code + lax.axis_index("code")).astype(jnp.int32).reshape(1)
    per = shard // code
    piece = lax.dynamic_slice_in_dim(embedding_vectors, lax.axis_index("code") * per, per, 0)
    pieces = gather_pieces(piece, size)
    params = pltpu.CompilerParams(vmem_limit_bytes=VMEM_LIMIT, dimension_semantics=("arbitrary",))
    kb = min(256, kl)
    x, peak, lse = pl.pallas_call(
        functools.partial(exponent_body, size=size, code=code, kb=kb),
        grid_spec=pltpu.PrefetchScalarGridSpec(
            num_scalar_prefetch=1,
            grid=(rows,),
            in_specs=[full((size, per, d)), full((kl, d))],
            out_specs=[
                pl.BlockSpec((kl, shard), lambda i, *_: (0, i)),
                pl.BlockSpec((1, 1, shard), lambda i, *_: (i, 0, 0)),
                pl.BlockSpec((1, 1, shard), lambda i, *_: (i, 0, 0)),
            ],
            scratch_shapes=[pltpu.VMEM((kl, shard), jnp.float32)],
        ),
        out_shape=[
            jax.ShapeDtypeStruct((kl, n), jnp.bfloat16),
            jax.ShapeDtypeStruct((rows, 1, shard), jnp.float32),
            jax.ShapeDtypeStruct((rows, 1, shard), jnp.float32),
        ],
        compiler_params=params,
        name="exponents",
    )(me, pieces, codebook)

    got, w = share_first(lse.reshape(nt, LANES), weights, nt, rows, code)
    peak = peak.reshape(nt, LANES)
    steps = kl // kb
    copies = copies_of(size, nt)
    vec = jax.ShapeDtypeStruct((nt, LANES), jnp.float32)
    factor = None
    for it in range(ITERS):
        first = it == 0
        out_specs = [pl.BlockSpec((1, kb), lambda i: (0, i)), full((copies, nt, LANES))]
        out_shape = [jax.ShapeDtypeStruct((1, kl), jnp.float32), jax.ShapeDtypeStruct((copies, nt, LANES), jnp.bfloat16)]
        if first:
            out_specs.append(full((nt, LANES)))
            out_shape.append(vec)
        res = pl.pallas_call(
            functools.partial(iterate_body, first=first, balance=balance),
            grid=(steps,),
            in_specs=[full(got.shape), full((nt, LANES)), full((nt, LANES)), pl.BlockSpec((kb, n), lambda i: (i, 0))],
            out_specs=out_specs,
            out_shape=out_shape,
            scratch_shapes=[
                pltpu.VMEM((16, n), jnp.bfloat16),
                pltpu.VMEM((8, n), jnp.float32),
                pltpu.VMEM((nt, LANES), jnp.float32),
            ],
            compiler_params=params,
            name="iterate",
        )(got, peak if first else factor, w, x)
        col, send = res[0], res[1]
        if first:
            factor = res[2]
        got = share(send)

    grad, load = pl.pallas_call(
        functools.partial(final_body, size=size, code=code, rows=rows, balance=balance),
        grid_spec=pltpu.PrefetchScalarGridSpec(
            num_scalar_prefetch=1,
            grid=(steps,),
            in_specs=[
                full(got.shape),
                full((nt, LANES)),
                full((nt, LANES)),
                pl.BlockSpec((kb, n), lambda i, *_: (i, 0)),
                pl.BlockSpec((1, kb), lambda i, *_: (0, i)),
                full((size, per, d)),
                pl.BlockSpec((kb, d), lambda i, *_: (i, 0)),
            ],
            out_specs=[pl.BlockSpec((kb, d), lambda i, *_: (i, 0)), pl.BlockSpec((1, kb), lambda i, *_: (0, i))],
            scratch_shapes=[pltpu.VMEM((16, n), jnp.bfloat16), pltpu.VMEM((n, d), jnp.bfloat16)],
        ),
        out_shape=[jax.ShapeDtypeStruct((kl, d), jnp.float32), jax.ShapeDtypeStruct((1, kl), jnp.float32)],
        compiler_params=params,
        name="finish",
    )(me, got, factor, w, x, col, pieces, codebook)
    return grad, load.reshape(kl)


def solution(mesh):
    placed = (P("rows", None), P(("code", "rows"), None), P("rows"))
    return jax.shard_map(
        local,
        mesh=mesh,
        in_specs=placed,
        out_specs=(P(("code", "rows"), None), P(("code", "rows"))),
        check_vma=False,
    )
```

```python
import functools

import jax
import jax.numpy as jnp
from jax import lax
from jax.experimental import pallas as pl
from jax.experimental.pallas import tpu as pltpu
from jax.sharding import PartitionSpec as P

ITERS = 3
SHARP = 2.0
LOG2E = 1.4426950408889634
AXES = ("rows", "code")
LANES = 128
VMEM_LIMIT = 32 * 1024 * 1024
NT = (((1,), (1,)), ((), ()))
NN = (((1,), (0,)), ((), ()))


def bit_groups(size):
    bits = [1 << b for b in range(size.bit_length() - 1)][::-1]
    return [tuple(bits[i : i + 2]) for i in range(0, len(bits), 2)]


def exchange(x, mask, size):
    return lax.ppermute(x, AXES, [(i, i ^ mask) for i in range(size)])


def gather_pieces(piece, size):
    out = piece[None]
    for group in bit_groups(size):
        masks = group if len(group) == 1 else (group[1], group[0], group[0] ^ group[1])
        out = jnp.concatenate([out] + [exchange(out, m, size) for m in masks], axis=0)
    return out


def slot_of(distance, size):
    slot, place = 0, 1
    for group in bit_groups(size):
        for bit in group[::-1]:
            slot = slot + jnp.where((distance & bit) != 0, place, 0)
            place *= 2
    return slot


def split2(x):
    hi = x.astype(jnp.bfloat16)
    lo = (x - hi.astype(jnp.float32)).astype(jnp.bfloat16)
    return hi, lo


def load_block(me_ref, pieces_ref, block, size, code):
    me = me_ref[0]
    parts = []
    for c in range(code):
        parts.append(pieces_ref[slot_of(me ^ (block * code + c), size)])
    return jnp.concatenate(parts, axis=0)


def exponent_body(me_ref, pieces_ref, book_ref, w_ref, x_ref, peak_ref, send_ref, scores, lse, *, size, code, rows, kb):
    shard = pieces_ref.shape[1] * code
    wide = shard // LANES
    kl = book_ref.shape[0]
    scale = SHARP * LOG2E

    def score(block, slot):
        e = load_block(me_ref, pieces_ref, block, size, code)
        peak = jnp.full((8, shard), -jnp.inf, jnp.float32)
        for k in range(0, kl, kb):
            s = lax.dot_general(book_ref[k : k + kb, :], e, NT, preferred_element_type=jnp.float32)
            scores[slot, k : k + kb, :] = s
            peak = jnp.maximum(peak, jnp.max(s.reshape(kb // 8, 8, shard), axis=0))
        return jnp.max(peak, axis=0, keepdims=True)

    def exponents(block, slot, peak):
        total = jnp.zeros((8, shard), jnp.float32)
        lanes = pl.ds(pl.multiple_of(block * shard, LANES), shard)
        for k in range(0, kl, kb):
            e = jnp.exp2((scores[slot, k : k + kb, :] - peak) * scale)
            x_ref[k : k + kb, lanes] = e.astype(jnp.bfloat16)
            total = total + jnp.sum(e.reshape(kb // 8, 8, shard), axis=0)
        total = jnp.sum(total, axis=0, keepdims=True)
        p = peak * SHARP
        l = p + jnp.log(total)
        for t in range(wide):
            peak_ref[pl.ds(block * wide + t, 1), :] = p[:, t * LANES : (t + 1) * LANES]
            lse[pl.ds(block * wide + t, 1), :] = l[:, t * LANES : (t + 1) * LANES]

    def pair(i, peak0):
        block = 2 * i
        peak1 = score(block + 1, 1)
        exponents(block, 0, peak0)
        peak0 = score(jnp.minimum(block + 2, rows - 1), 0)
        exponents(block + 1, 1, peak1)
        return peak0

    lax.fori_loop(0, rows // 2, pair, score(0, 0))
    nt = rows * wide
    copies = send_ref.shape[0]
    send_ref[:, :nt, :] = jnp.broadcast_to(lse[...][None], (copies, nt, LANES))
    for t in range(wide):
        send_ref[:, nt + t : nt + t + 1, :] = jnp.broadcast_to(w_ref[:, t * LANES : (t + 1) * LANES][None], (copies, 1, LANES))


def row_factor(first, got_ref, peak_ref, w_ref, factor_ref, nt):
    if first:
        got = got_ref[:, :nt, :]
        top = jnp.max(got, axis=0)
        common = top + jnp.log(jnp.sum(jnp.exp(got - top[None]), axis=0))
        factor = jnp.exp(peak_ref[...] - common)
        return w_ref[...] * factor, factor
    total = jnp.sum(got_ref[...].astype(jnp.float32), axis=0)
    factor = factor_ref[...]
    return w_ref[...] / total * factor, factor


def put_rows(lhs, r, n):
    hi, lo = split2(r)
    for t in range(n // LANES):
        lhs[0:8, t * LANES : (t + 1) * LANES] = jnp.broadcast_to(r[t : t + 1, :], (8, LANES)).astype(jnp.bfloat16)
        lhs[8:16, t * LANES : (t + 1) * LANES] = jnp.broadcast_to(
            r[t : t + 1, :] - hi[t : t + 1, :].astype(jnp.float32), (8, LANES)
        ).astype(jnp.bfloat16)


def iterate_body(*refs, first, balance, code, kb):
    if first:
        got_ref, peak_ref, w_in, x_ref, col_ref, send_ref, factor_ref, w_ref, lhs = refs
        nt = peak_ref.shape[0]
        if w_in is None or got_ref.shape[0] > 1:
            wt = got_ref.shape[1] - nt
            for b in range(nt // wt):
                w_ref[b * wt : (b + 1) * wt, :] = got_ref[b * code, nt:, :]
        else:
            w_ref[...] = w_in[...]
    else:
        got_ref, factor_ref, w_ref, x_ref, col_ref, send_ref, lhs = refs
        peak_ref = None
    nt = factor_ref.shape[0]
    n = nt * LANES
    kl = x_ref.shape[0]
    r, factor = row_factor(first, got_ref, peak_ref, w_ref, factor_ref, nt)
    if first:
        factor_ref[...] = factor
    put_rows(lhs, r, n)
    acc = jnp.zeros((16, n), jnp.float32)
    for k in range(0, kl, kb):
        x = x_ref[k : k + kb, :]
        cols = lax.dot_general(lhs[...], x, NT, preferred_element_type=jnp.float32)
        col = balance / (cols[0:1] + cols[8:9])
        col_ref[:, k : k + kb] = col
        hi, lo = split2(jnp.broadcast_to(col, (8, kb)))
        acc = acc + lax.dot_general(jnp.concatenate([hi, lo], axis=0), x, NN, preferred_element_type=jnp.float32)
    sums = acc[0:1] + acc[8:9]
    for t in range(nt):
        part = sums[:, t * LANES : (t + 1) * LANES] * factor[t : t + 1, :]
        send_ref[:, t : t + 1, :] = jnp.broadcast_to(part.astype(jnp.bfloat16)[None], (send_ref.shape[0], 1, LANES))


def final_body(me_ref, got_ref, factor_ref, w_ref, x_ref, col_ref, pieces_ref, book_ref, grad_ref, load_ref, lhs, weighted, rt, stage, sems, *, size, code, rows, balance, kb):
    nt = w_ref.shape[0]
    n = nt * LANES
    r, _ = row_factor(False, got_ref, None, w_ref, factor_ref, nt)
    put_rows(lhs, r, n)
    wide = nt // rows
    rt[...] = r.reshape(rows, wide, LANES)

    def weigh(b, _):
        block = load_block(me_ref, pieces_ref, b, size, code)
        cols = jnp.concatenate([rt[b], jnp.zeros((8 - wide % 8, LANES), jnp.float32)], axis=0).T
        for t in range(wide):
            scaled = block[t * LANES : (t + 1) * LANES, :].astype(jnp.float32) * cols[:, t : t + 1]
            weighted[pl.ds(pl.multiple_of((b * wide + t) * LANES, LANES), LANES), :] = scaled.astype(jnp.bfloat16)
        return 0

    lax.fori_loop(0, rows, weigh, 0, unroll=min(rows, 4))
    kl = x_ref.shape[0]
    copies = []
    for i, k in enumerate(range(0, kl, kb)):
        x = x_ref[k : k + kb, :]
        cols = lax.dot_general(lhs[...], x, NT, preferred_element_type=jnp.float32)
        col = col_ref[:, k : k + kb]
        mass = col * (cols[0:1] + cols[8:9]) / balance
        load_ref[:, k : k + kb] = mass
        both = jnp.concatenate([mass, col / balance, jnp.zeros((6, kb), jnp.float32)], axis=0).T
        sums = jnp.dot(x, weighted[...], preferred_element_type=jnp.float32)
        stage[k : k + kb, :] = both[:, 0:1] * book_ref[k : k + kb, :].astype(jnp.float32) - both[:, 1:2] * sums
        copy = pltpu.make_async_copy(stage.at[k : k + kb, :], grad_ref.at[k : k + kb, :], sems.at[i])
        copy.start()
        copies.append(copy)
    for copy in copies:
        copy.wait()


def share_first(send, weights, nt):
    if send.shape[0] == 1:
        lse = send[0, :nt, :]
        top = lax.pmax(lse, AXES)
        common = top + jnp.log(lax.psum(jnp.exp(lse - top), AXES))
        return common[None], lax.all_gather(weights, "rows", axis=0, tiled=True).reshape(nt, LANES)
    got = lax.all_to_all(send, AXES, split_axis=0, concat_axis=0, tiled=True)
    return got, jnp.zeros((8, LANES), jnp.float32)


def share(send):
    if send.shape[0] == 1:
        return lax.psum(send.astype(jnp.float32), AXES)
    return lax.all_to_all(send, AXES, split_axis=0, concat_axis=0, tiled=True)


def copies_of(size, nt):
    return size if size * nt * LANES <= 1 << 20 else 1


IN_VMEM = pl.BlockSpec(memory_space=pltpu.VMEM)
IN_SMEM = pl.BlockSpec(memory_space=pltpu.SMEM)


def call(body, name, args, outs, scratch, out_specs=None):
    return pl.pallas_call(
        body,
        in_specs=[IN_SMEM if a.dtype == jnp.int32 else IN_VMEM for a in args],
        out_specs=out_specs or [IN_VMEM] * len(outs),
        out_shape=outs,
        scratch_shapes=scratch,
        compiler_params=pltpu.CompilerParams(vmem_limit_bytes=VMEM_LIMIT),
        name=name,
    )(*args)


def local(embedding_vectors, codebook, weights):
    rows, code = lax.axis_size("rows"), lax.axis_size("code")
    size = rows * code
    shard, d = embedding_vectors.shape
    kl = codebook.shape[0]
    n = rows * shard
    nt = n // LANES
    wt = shard // LANES
    balance = n / (size * kl)
    copies = copies_of(size, nt)
    me = (lax.axis_index("rows") * code + lax.axis_index("code")).astype(jnp.int32).reshape(1)
    per = shard // code
    piece = lax.dynamic_slice_in_dim(embedding_vectors, lax.axis_index("code") * per, per, 0)
    pieces = gather_pieces(piece, size)
    vec = jax.ShapeDtypeStruct((nt, LANES), jnp.float32)
    lhs = pltpu.VMEM((16, n), jnp.bfloat16)
    kb = min(512, kl)
    x, peak, send = call(
        functools.partial(exponent_body, size=size, code=code, rows=rows, kb=min(256, kl)),
        "exponents",
        (me, pieces, codebook, weights.reshape(1, shard)),
        [pltpu.VMEM((kl, n), jnp.bfloat16), vec, jax.ShapeDtypeStruct((copies, nt + wt, LANES), jnp.float32)],
        [pltpu.VMEM((2, kl, shard), jnp.float32), pltpu.VMEM((nt, LANES), jnp.float32)],
    )
    x = pltpu.with_memory_space_constraint(x, pltpu.VMEM)
    got, w = share_first(send, weights, nt)
    messages = jax.ShapeDtypeStruct((copies, nt, LANES), jnp.bfloat16)
    columns = jax.ShapeDtypeStruct((1, kl), jnp.float32)
    body = functools.partial(iterate_body, balance=balance, code=code, kb=kb)
    col, send, factor, w = call(functools.partial(body, first=True), "iterate_first", (got, peak, w, x), [columns, messages, vec, vec], [lhs])
    got = share(send)
    for _ in range(ITERS - 1):
        col, send = call(functools.partial(body, first=False), "iterate", (got, factor, w, x), [columns, messages], [lhs])
        got = share(send)
    steps = kl // kb
    grad, load = call(
        functools.partial(final_body, size=size, code=code, rows=rows, balance=balance, kb=kb),
        "finish",
        (me, got, factor, w, x, col, pieces, codebook),
        [jax.ShapeDtypeStruct((kl, d), jnp.float32), columns],
        [
            lhs,
            pltpu.VMEM((n, d), jnp.bfloat16),
            pltpu.VMEM((rows, wt, LANES), jnp.float32),
            pltpu.VMEM((kl, d), jnp.float32),
            pltpu.SemaphoreType.DMA((steps,)),
        ],
        [pl.BlockSpec(memory_space=pl.ANY), IN_VMEM],
    )
    return grad, load.reshape(kl)


def solution(mesh):
    placed = (P("rows", None), P(("code", "rows"), None), P("rows"))
    return jax.shard_map(
        local,
        mesh=mesh,
        in_specs=placed,
        out_specs=(P(("code", "rows"), None), P(("code", "rows"))),
        check_vma=False,
    )
```

```python
import functools

import jax
import jax.numpy as jnp
import numpy as np
from jax import lax
from jax.experimental import pallas as pl
from jax.experimental.pallas import tpu as pltpu
from jax.sharding import PartitionSpec as P

ITERS = 3
SHARP = 2.0
LOG2E = 1.4426950408889634
AXES = ("rows", "code")
MANY = 64
LANES = 128
VMEM_LIMIT = 32 * 1024 * 1024
NT = (((1,), (1,)), ((), ()))
NN = (((1,), (0,)), ((), ()))


def bit_groups(size):
    bits = [1 << b for b in range(size.bit_length() - 1)][::-1]
    return [tuple(bits[i : i + 2]) for i in range(0, len(bits), 2)]


def exchange(x, mask, size):
    return lax.ppermute(x, AXES, [(i, i ^ mask) for i in range(size)])


def gather_blocks(piece, size):
    groups = bit_groups(size)
    segments = None
    for i, group in enumerate(groups):
        masks = group if len(group) == 1 else (group[1], group[0], group[0] ^ group[1])
        if segments is None:
            first = piece[None]
            segments = [jnp.concatenate([first] + [exchange(first, m, size) for m in masks], axis=0)[None]]
        else:
            if size > MANY:
                segments = [jnp.concatenate(segments, axis=0)]
            segments = segments + [exchange(x, m, size) for m in masks for x in segments]
    return segments if size <= MANY else [jnp.concatenate(segments, axis=0)]


def slot_of(device, size):
    slot, place = 0, 1
    for group in bit_groups(size):
        for bit in group[::-1]:
            slot = slot + jnp.where((device & bit) != 0, place, 0)
            place *= 2
    return slot


def split2(x):
    hi = x.astype(jnp.bfloat16)
    lo = (x - hi.astype(jnp.float32)).astype(jnp.bfloat16)
    return hi, lo


def load_block(segments, block, mine):
    count = segments[0].shape[0]
    ref, at = (segments[block], 0) if count == 1 else (segments[0], block)
    return jnp.concatenate([ref[at, j ^ mine] for j in range(ref.shape[1])], axis=0)


def exponent_body(*refs, size, code, first, start, through, kb):
    n_in = len(refs) - 4 - through - (0 if first else 3)
    me_ref, w_ref, book_ref, segments = refs[0], refs[1], refs[2], refs[3:n_in]
    x_ref, peak_ref, lse_ref = refs[len(refs) - 4 - through : len(refs) - 1 - through]
    scores = refs[-1]
    fan, per = segments[0].shape[1:3]
    shard = fan * per
    wide = shard // LANES
    kl = book_ref.shape[0]
    scale = SHARP * LOG2E
    slot = slot_of(me_ref[0], size)
    mine, home = slot & (fan - 1), slot // fan
    count = max(len(segments), segments[0].shape[0])
    if first and fan == code:
        lane = lax.broadcasted_iota(jnp.int32, (8, shard), 1) // per
        moved = pltpu.roll(jnp.broadcast_to(w_ref[...].reshape(1, shard), (8, shard)), ((mine - (me_ref[0] & (code - 1))) & (code - 1)) * per, 1)
        moved = jnp.where(lane == mine, moved, 0.0)
        for t in range(wide):
            lse_ref[lse_ref.shape[0] - wide + t : lse_ref.shape[0] - wide + t + 1, :] = moved[0:1, t * LANES : (t + 1) * LANES]

    def score(block, at):
        e = load_block(segments, block, mine)
        peak = jnp.full((8, shard), -jnp.inf, jnp.float32)
        for k in range(0, kl, kb):
            s = lax.dot_general(book_ref[k : k + kb, :], e, NT, preferred_element_type=jnp.float32)
            scores[at, k : k + kb, :] = s
            peak = jnp.maximum(peak, jnp.max(s.reshape(kb // 8, 8, shard), axis=0))
        return jnp.max(peak, axis=0, keepdims=True)

    def exponents(block, at, peak):
        block = (start[block] if isinstance(block, int) else block) ^ home
        total = jnp.zeros((8, shard), jnp.float32)
        lanes = pl.ds(pl.multiple_of(block * shard, LANES), shard)
        for k in range(0, kl, kb):
            e = jnp.exp2((scores[at, k : k + kb, :] - peak) * scale)
            x_ref[k : k + kb, lanes] = e.astype(jnp.bfloat16)
            total = total + jnp.sum(e.reshape(kb // 8, 8, shard), axis=0)
        total = jnp.sum(total, axis=0, keepdims=True)
        p = peak * SHARP
        l = p + jnp.log(total)
        for t in range(wide):
            peak_ref[pl.ds(block * wide + t, 1), :] = p[:, t * LANES : (t + 1) * LANES]
            lse_ref[pl.ds(block * wide + t, 1), :] = l[:, t * LANES : (t + 1) * LANES]

    if len(segments) == count:
        peak = score(0, 0)
        for i in range(count):
            following = score(i + 1, (i + 1) % 2) if i + 1 < count else None
            exponents(i, i % 2, peak)
            peak = following
        return

    def pair(i, peak0):
        peak1 = score(2 * i + 1, 1)
        exponents(2 * i, 0, peak0)
        peak0 = score(jnp.minimum(2 * i + 2, count - 1), 0)
        exponents(2 * i + 1, 1, peak1)
        return peak0

    lax.fori_loop(0, count // 2, pair, score(0, 0))


def row_factor(first, got_ref, peak_ref, w_ref, factor_ref, nt):
    if first:
        got = got_ref[:, :nt, :]
        top = jnp.max(got, axis=0)
        common = top + jnp.log(jnp.sum(jnp.exp(got - top[None]), axis=0))
        factor = jnp.exp(peak_ref[...] - common)
        return w_ref[...] * factor, factor
    total = jnp.sum(got_ref[...].astype(jnp.float32), axis=0)
    factor = factor_ref[...]
    return w_ref[...] / total * factor, factor


def put_rows(dst, r):
    for t in range(r.shape[0]):
        dst[:, t * LANES : (t + 1) * LANES] = jnp.broadcast_to(r[t : t + 1, :], (8, LANES))


def column_sums(x_ref, r_ref, k, kb):
    parts = []
    for g in range(k, k + kb, 16):
        sums = [None, None]
        for t in range(r_ref.shape[1] // LANES):
            lanes = slice(t * LANES, (t + 1) * LANES)
            term = x_ref[g : g + 16, lanes].astype(jnp.float32) * jnp.broadcast_to(r_ref[0:1, lanes], (16, LANES))
            sums[t % 2] = term if sums[t % 2] is None else sums[t % 2] + term
        parts.append(sums[0] + sums[1])
    return jnp.sum(jnp.concatenate(parts, axis=0).T, axis=0, keepdims=True)


def iterate_body(*refs, first, balance, kb, plan):
    if first:
        got_ref, peak_ref, x_ref = refs[:3]
        col_ref, send_ref, factor_ref, w_ref, r_rows, acc = refs[-6:]
        nt = peak_ref.shape[0]
        if plan is None:
            w_ref[...] = refs[3][...]
        else:
            wide = (got_ref.shape[1] - nt) // 2
            for b, sources in enumerate(plan):
                parts = [got_ref[i, nt + wide * c : nt + wide * (c + 1), :] for i, c in sources]
                w_ref[b * wide : (b + 1) * wide, :] = functools.reduce(jnp.add, parts)
    else:
        got_ref, factor_ref, w_ref, x_ref, col_ref, send_ref, r_rows, acc = refs
        peak_ref = None
    nt = factor_ref.shape[0]
    n = nt * LANES
    kl = x_ref.shape[0]
    r, factor = row_factor(first, got_ref, peak_ref, w_ref, factor_ref, nt)
    if first:
        factor_ref[...] = factor
    put_rows(r_rows, r)
    acc[...] = jnp.zeros(acc.shape, jnp.float32)

    def add_rows(k, col):
        hi, lo = split2(jnp.broadcast_to(col, (8, kb)))
        acc[...] += jnp.dot(jnp.concatenate([hi, lo], axis=0), x_ref[k : k + kb, :], preferred_element_type=jnp.float32)

    before = None
    for k in range(0, kl, kb):
        col = balance / column_sums(x_ref, r_rows, k, kb)
        col_ref[:, k : k + kb] = col
        if before is not None:
            add_rows(k - kb, before)
        before = col
    add_rows(kl - kb, before)
    sums = acc[0:1, :] + acc[8:9, :]
    for t in range(nt):
        part = sums[:, t * LANES : (t + 1) * LANES] * factor[t : t + 1, :]
        send_ref[:, t : t + 1, :] = jnp.broadcast_to(part.astype(jnp.bfloat16)[None], (send_ref.shape[0], 1, LANES))


def final_body(*refs, size, balance, kb):
    me_ref, got_ref, factor_ref, w_ref, x_ref, col_ref, book_ref = refs[:7]
    segments = refs[7:-7]
    grad_ref, load_ref, r_rows, weighted, rt, stage, sems = refs[-7:]
    nt = w_ref.shape[0]
    n = nt * LANES
    r, _ = row_factor(False, got_ref, None, w_ref, factor_ref, nt)
    put_rows(r_rows, r)
    fan, per = segments[0].shape[1:3]
    wide = fan * per // LANES
    blocks = nt // wide
    rt[...] = r.reshape(blocks, wide, LANES)
    slot = slot_of(me_ref[0], size)
    mine, home = slot & (fan - 1), slot // fan

    def weigh(i, _):
        block = load_block(segments, i, mine)
        b = i ^ home
        cols = jnp.concatenate([rt[b], jnp.zeros((8 - wide % 8, LANES), jnp.float32)], axis=0).T
        for t in range(wide):
            scaled = block[t * LANES : (t + 1) * LANES, :].astype(jnp.float32) * cols[:, t : t + 1]
            weighted[pl.ds(pl.multiple_of((b * wide + t) * LANES, LANES), LANES), :] = scaled.astype(jnp.bfloat16)
        return 0

    if len(segments) == blocks:
        for i in range(blocks):
            weigh(i, 0)
    else:
        lax.fori_loop(0, blocks, weigh, 0)
    kl = x_ref.shape[0]
    copies = []
    for i, k in enumerate(range(0, kl, kb)):
        x = x_ref[k : k + kb, :]
        col = col_ref[:, k : k + kb]
        mass = col * column_sums(x_ref, r_rows, k, kb) / balance
        load_ref[:, k : k + kb] = mass
        both = jnp.concatenate([mass, col / balance, jnp.zeros((6, kb), jnp.float32)], axis=0).T
        sums = jnp.dot(x, weighted[...], preferred_element_type=jnp.float32)
        stage[k : k + kb, :] = both[:, 0:1] * book_ref[k : k + kb, :].astype(jnp.float32) - both[:, 1:2] * sums
        copy = pltpu.make_async_copy(stage.at[k : k + kb, :], grad_ref.at[k : k + kb, :], sems.at[i])
        copy.start()
        copies.append(copy)
    for copy in copies:
        copy.wait()


def join_body(me_ref, own_ref, other_ref, out_ref, *, nt):
    wide = own_ref.shape[0] - nt
    copies = out_ref.shape[0]
    a, b = own_ref[:nt, :], other_ref[:nt, :]
    top = jnp.maximum(a, b)
    joined = top + jnp.log(jnp.exp(a - top) + jnp.exp(b - top))
    out_ref[:, :nt, :] = jnp.broadcast_to(joined[None], (copies, nt, LANES))
    odd = (me_ref[0] & 1) == 1
    a, b = own_ref[nt:, :], other_ref[nt:, :]
    out_ref[:, nt : nt + wide, :] = jnp.broadcast_to(jnp.where(odd, b, a)[None], (copies, wide, LANES))
    out_ref[:, nt + wide :, :] = jnp.broadcast_to(jnp.where(odd, a, b)[None], (copies, wide, LANES))


def share_first(lse, weights, me1, size, copies, nt):
    shard = weights.shape[0]
    code = lax.axis_size("code")
    groups = bit_groups(size)
    fan = 1 << len(groups[0])
    if copies == 1:
        lse = lse[:nt]
        top = lax.pmax(lse, AXES)
        common = top + jnp.log(lax.psum(jnp.exp(lse - top), AXES))
        w = lax.all_gather(weights, "rows", axis=0, tiled=True).reshape(size, shard // code)
        order = np.argsort([slot_int(g, size) for g in range(size)])
        return common[None], w[order].reshape(nt, LANES), None
    other = exchange(lse, 1, size)
    wide = lse.shape[0] - nt
    (message,) = call(
        functools.partial(join_body, nt=nt),
        "join",
        (me1, lse, other),
        [jax.ShapeDtypeStruct((size // 2, nt + 2 * wide, LANES), jnp.float32)],
        [],
    )
    same = [[i for i in range(size) if i % 2 == c] for c in range(2)]
    got = lax.all_to_all(message, AXES, split_axis=0, concat_axis=0, tiled=True, axis_index_groups=same)
    plan = [[] for _ in range(size // fan)]
    for g in range(size):
        plan[slot_int(g, size) // fan].append((g // 2, g % 2))
    return got, None, plan


def slot_int(device, size):
    bits = [bit for group in bit_groups(size) for bit in group[::-1]]
    return sum(1 << i for i, bit in enumerate(bits) if device & bit)


def share(send):
    if send.shape[0] == 1:
        return lax.psum(send.astype(jnp.float32), AXES)
    return lax.all_to_all(send, AXES, split_axis=0, concat_axis=0, tiled=True)


def copies_of(size, nt):
    return size if size * nt * LANES <= 1 << 20 else 1


IN_VMEM = pl.BlockSpec(memory_space=pltpu.VMEM)
IN_SMEM = pl.BlockSpec(memory_space=pltpu.SMEM)


def call(body, name, args, outs, scratch, out_specs=None, aliases=None, cost=None):
    return pl.pallas_call(
        body,
        in_specs=[IN_SMEM if a.dtype == jnp.int32 else IN_VMEM for a in args],
        out_specs=out_specs or [IN_VMEM] * len(outs),
        out_shape=outs,
        scratch_shapes=scratch,
        input_output_aliases=aliases or {},
        cost_estimate=cost,
        compiler_params=pltpu.CompilerParams(vmem_limit_bytes=VMEM_LIMIT),
        name=name,
    )(*args)


def local(embedding_vectors, codebook, weights):
    rows, code = lax.axis_size("rows"), lax.axis_size("code")
    size = rows * code
    shard, d = embedding_vectors.shape
    kl = codebook.shape[0]
    n = rows * shard
    nt = n // LANES
    balance = n / (size * kl)
    copies = copies_of(size, nt)
    me = (lax.axis_index("rows") * code + lax.axis_index("code")).astype(jnp.int32)
    per = shard // code
    piece = lax.dynamic_slice_in_dim(embedding_vectors, lax.axis_index("code") * per, per, 0)
    me1 = me.reshape(1)
    vec = jax.ShapeDtypeStruct((nt, LANES), jnp.float32)
    outs = [pltpu.VMEM((kl, n), jnp.bfloat16), pltpu.VMEM((nt, LANES), jnp.float32)]
    outs.append(pltpu.VMEM((nt + shard // LANES, LANES), jnp.float32))
    block = per << len(bit_groups(size)[0])

    def exponents(state, chosen, part, through=0):
        state = tuple(pltpu.with_memory_space_constraint(a, pltpu.VMEM) for a in state)
        args = (me1, weights, book, *part) + state
        count = sum(p.shape[0] for p in part)
        aliases = {3 + i: 3 + i for i in range(through)}
        if state:
            aliases.update({len(args) - 3 + i: i for i in range(3)})
        out = call(
            functools.partial(exponent_body, size=size, code=code, first=not state, start=chosen, through=through, kb=min(256, kl)),
            "exponents",
            args,
            outs + [jax.ShapeDtypeStruct(p.shape, p.dtype) for p in part[:through]],
            [pltpu.VMEM((2, kl, block), jnp.float32)],
            cost=pl.CostEstimate(
                flops=2 * kl * d * block * count, transcendentals=kl * block * count, bytes_accessed=6 * kl * block * count
            ),
            aliases=aliases,
        )
        return tuple(out[:3]), out[3:]

    book = pltpu.with_memory_space_constraint(codebook, pltpu.VMEM)
    if size == 32:
        first = piece[None]
        a0 = jnp.concatenate([first] + [exchange(first, m, size) for m in (8, 16, 24)], axis=0)[None]
        a1 = exchange(a0, 1, size)
        x0, y0, d0 = (exchange(a0, m, size) for m in (2, 4, 6))
        state, _ = exponents((), [0, 4], [a0, a1])
        state, (x0, y0) = exponents(state, [1, 2], [x0, y0], 2)
        x1, y1 = exchange(x0, 1, size), exchange(y0, 1, size)
        state, (d0,) = exponents(state, [3], [d0], 1)
        d1 = exchange(d0, 1, size)
        state, _ = exponents(state, [5, 6], [x1, y1])
        state, _ = exponents(state, [7], [d1])
        segments = [a0, x0, y0, d0, a1, x1, y1, d1]
    else:
        segments = gather_blocks(piece, size)
        state, _ = exponents((), list(range(len(segments))), segments)
    x, peak, lse = state
    x = pltpu.with_memory_space_constraint(x, pltpu.VMEM)
    got, w, plan = share_first(lse, weights, me1, size, copies, nt)
    rows_f32 = pltpu.VMEM((8, n), jnp.float32)
    kb = min(256, kl)
    scratch = [rows_f32, pltpu.VMEM((16, n), jnp.float32)]
    messages = jax.ShapeDtypeStruct((copies, nt, LANES), jnp.bfloat16)
    columns = jax.ShapeDtypeStruct((1, kl), jnp.float32)
    body = functools.partial(iterate_body, balance=balance, kb=kb, plan=plan)
    col, send, factor, w = call(functools.partial(body, first=True), "iterate_first", (got, peak, x) + (() if w is None else (w,)), [columns, messages, vec, vec], scratch)
    got = share(send)
    for _ in range(ITERS - 1):
        col, send = call(functools.partial(body, first=False), "iterate", (got, factor, w, x), [columns, messages], scratch)
        got = share(send)
    grad, load = call(
        functools.partial(final_body, size=size, balance=balance, kb=kb),
        "finish",
        (me1, got, factor, w, x, col, codebook, *segments),
        [jax.ShapeDtypeStruct((kl, d), jnp.float32), columns],
        [
            rows_f32,
            pltpu.VMEM((n, d), jnp.bfloat16),
            pltpu.VMEM((n // block, block // LANES, LANES), jnp.float32),
            pltpu.VMEM((kl, d), jnp.float32),
            pltpu.SemaphoreType.DMA((kl // kb,)),
        ],
        [pl.BlockSpec(memory_space=pl.ANY), IN_VMEM],
    )
    return grad, load.reshape(kl)


def solution(mesh):
    placed = (P("rows", None), P(("code", "rows"), None), P("rows"))
    return jax.shard_map(
        local,
        mesh=mesh,
        in_specs=placed,
        out_specs=(P(("code", "rows"), None), P(("code", "rows"))),
        check_vma=False,
    )
```

```python
import functools

import jax
import jax.numpy as jnp
import numpy as np
from jax import lax
from jax.experimental import pallas as pl
from jax.experimental.pallas import tpu as pltpu
from jax.sharding import PartitionSpec as P

ITERS = 3
SHARP = 2.0
LOG2E = 1.4426950408889634
AXES = ("rows", "code")
MANY = 64
LANES = 128
VMEM_LIMIT = 32 * 1024 * 1024
NT = (((1,), (1,)), ((), ()))
NN = (((1,), (0,)), ((), ()))


def bit_groups(size):
    bits = [1 << b for b in range(size.bit_length() - 1)][::-1]
    return [tuple(bits[i : i + 2]) for i in range(0, len(bits), 2)]


def exchange(x, mask, size):
    return lax.ppermute(x, AXES, [(i, i ^ mask) for i in range(size)])


def gather_blocks(piece, size):
    groups = bit_groups(size)
    segments = None
    for i, group in enumerate(groups):
        masks = group if len(group) == 1 else (group[1], group[0], group[0] ^ group[1])
        if segments is None:
            first = piece[None]
            segments = [jnp.concatenate([first] + [exchange(first, m, size) for m in masks], axis=0)[None]]
        else:
            if size > MANY:
                segments = [jnp.concatenate(segments, axis=0)]
            segments = segments + [exchange(x, m, size) for m in masks for x in segments]
    return segments if size <= MANY else [jnp.concatenate(segments, axis=0)]


def slot_of(device, size):
    slot, place = 0, 1
    for group in bit_groups(size):
        for bit in group[::-1]:
            slot = slot + jnp.where((device & bit) != 0, place, 0)
            place *= 2
    return slot


def split2(x):
    hi = x.astype(jnp.bfloat16)
    lo = (x - hi.astype(jnp.float32)).astype(jnp.bfloat16)
    return hi, lo


def load_block(segments, block, mine):
    count = segments[0].shape[0]
    ref, at = (segments[block], 0) if count == 1 else (segments[0], block)
    return jnp.concatenate([ref[at, j ^ mine] for j in range(ref.shape[1])], axis=0)


def exponent_body(*refs, size, code, first, start, through, kb):
    n_in = len(refs) - 4 - through - (0 if first else 3)
    me_ref, w_ref, book_ref, segments = refs[0], refs[1], refs[2], refs[3:n_in]
    x_ref, peak_ref, lse_ref = refs[len(refs) - 4 - through : len(refs) - 1 - through]
    scores = refs[-1]
    fan, per = segments[0].shape[1:3]
    shard = fan * per
    wide = shard // LANES
    kl = book_ref.shape[0]
    scale = SHARP * LOG2E
    slot = slot_of(me_ref[0], size)
    mine, home = slot & (fan - 1), slot // fan
    count = max(len(segments), segments[0].shape[0])
    if first and fan == code:
        lane = lax.broadcasted_iota(jnp.int32, (8, shard), 1) // per
        moved = pltpu.roll(jnp.broadcast_to(w_ref[...].reshape(1, shard), (8, shard)), ((mine - (me_ref[0] & (code - 1))) & (code - 1)) * per, 1)
        moved = jnp.where(lane == mine, moved, 0.0)
        for t in range(wide):
            lse_ref[lse_ref.shape[0] - wide + t : lse_ref.shape[0] - wide + t + 1, :] = moved[0:1, t * LANES : (t + 1) * LANES]

    def score(block, at):
        e = load_block(segments, block, mine)
        peak = jnp.full((8, shard), -jnp.inf, jnp.float32)
        for k in range(0, kl, kb):
            s = lax.dot_general(book_ref[k : k + kb, :], e, NT, preferred_element_type=jnp.float32)
            scores[at, k : k + kb, :] = s
            peak = jnp.maximum(peak, jnp.max(s.reshape(kb // 8, 8, shard), axis=0))
        return jnp.max(peak, axis=0, keepdims=True)

    def exponents(block, at, peak):
        block = (start[block] if isinstance(block, int) else block) ^ home
        total = jnp.zeros((8, shard), jnp.float32)
        lanes = pl.ds(pl.multiple_of(block * shard, LANES), shard)
        for k in range(0, kl, kb):
            e = jnp.exp2((scores[at, k : k + kb, :] - peak) * scale)
            x_ref[k : k + kb, lanes] = e.astype(jnp.bfloat16)
            total = total + jnp.sum(e.reshape(kb // 8, 8, shard), axis=0)
        total = jnp.sum(total, axis=0, keepdims=True)
        p = peak * SHARP
        l = p + jnp.log(total)
        for t in range(wide):
            peak_ref[pl.ds(block * wide + t, 1), :] = p[:, t * LANES : (t + 1) * LANES]
            lse_ref[pl.ds(block * wide + t, 1), :] = l[:, t * LANES : (t + 1) * LANES]

    if len(segments) == count:
        peak = score(0, 0)
        for i in range(count):
            following = score(i + 1, (i + 1) % 2) if i + 1 < count else None
            exponents(i, i % 2, peak)
            peak = following
        return

    def pair(i, peak0):
        peak1 = score(2 * i + 1, 1)
        exponents(2 * i, 0, peak0)
        peak0 = score(jnp.minimum(2 * i + 2, count - 1), 0)
        exponents(2 * i + 1, 1, peak1)
        return peak0

    lax.fori_loop(0, count // 2, pair, score(0, 0))


def row_factor(first, got_ref, peak_ref, w_ref, factor_ref, nt):
    if first:
        got = got_ref[:, :nt, :]
        top = jnp.max(got, axis=0)
        common = top + jnp.log(jnp.sum(jnp.exp(got - top[None]), axis=0))
        factor = jnp.exp(peak_ref[...] - common)
        return w_ref[...] * factor, factor
    total = jnp.sum(got_ref[...].astype(jnp.float32), axis=0)
    factor = factor_ref[...]
    return w_ref[...] / total * factor, factor


def put_rows(dst, r):
    for t in range(r.shape[0]):
        dst[:, t * LANES : (t + 1) * LANES] = jnp.broadcast_to(r[t : t + 1, :], (16, LANES)).astype(jnp.bfloat16)


def column_sums(x_ref, r_ref, k, kb):
    tiles = r_ref.shape[1] // LANES
    join = 4 if tiles % 4 == 0 else 1
    parts = []
    for g in range(k, k + kb, 16):
        total = None
        for t in range(0, tiles, join):
            terms = []
            for u in range(t, t + join):
                lanes = slice(u * LANES, (u + 1) * LANES)
                terms.append(x_ref[g : g + 16, lanes] * r_ref[:, lanes])
            while len(terms) > 1:
                terms = [terms[i] + terms[i + 1] for i in range(0, len(terms), 2)]
            term = terms[0].astype(jnp.float32)
            total = term if total is None else total + term
        parts.append(total)
    return jnp.sum(jnp.concatenate(parts, axis=0).T, axis=0, keepdims=True)


def iterate_body(*refs, first, balance, kb, plan):
    if first:
        got_ref, peak_ref, x_ref = refs[:3]
        col_ref, send_ref, factor_ref, w_ref, r_rows, acc = refs[-6:]
        nt = peak_ref.shape[0]
        if plan is None:
            w_ref[...] = refs[3][...]
        else:
            wide = (got_ref.shape[1] - nt) // 2
            for b, sources in enumerate(plan):
                parts = [got_ref[i, nt + wide * c : nt + wide * (c + 1), :] for i, c in sources]
                w_ref[b * wide : (b + 1) * wide, :] = functools.reduce(jnp.add, parts)
    else:
        got_ref, factor_ref, w_ref, x_ref, col_ref, send_ref, r_rows, acc = refs
        peak_ref = None
    nt = factor_ref.shape[0]
    n = nt * LANES
    kl = x_ref.shape[0]
    r, factor = row_factor(first, got_ref, peak_ref, w_ref, factor_ref, nt)
    if first:
        factor_ref[...] = factor
    put_rows(r_rows, r)
    acc[...] = jnp.zeros(acc.shape, jnp.float32)

    def add_rows(k, col):
        hi, lo = split2(jnp.broadcast_to(col, (8, kb)))
        acc[...] += jnp.dot(jnp.concatenate([hi, lo], axis=0), x_ref[k : k + kb, :], preferred_element_type=jnp.float32)

    before = None
    for k in range(0, kl, kb):
        col = balance / column_sums(x_ref, r_rows, k, kb)
        col_ref[:, k : k + kb] = col
        if before is not None:
            add_rows(k - kb, before)
        before = col
    add_rows(kl - kb, before)
    sums = acc[0:1, :] + acc[8:9, :]
    for t in range(nt):
        part = sums[:, t * LANES : (t + 1) * LANES] * factor[t : t + 1, :]
        send_ref[:, t : t + 1, :] = jnp.broadcast_to(part.astype(jnp.bfloat16)[None], (send_ref.shape[0], 1, LANES))


def final_body(*refs, size, balance, kb):
    me_ref, got_ref, factor_ref, w_ref, x_ref, col_ref, book_ref = refs[:7]
    segments = refs[7:-7]
    grad_ref, load_ref, r_rows, weighted, rt, stage, sems = refs[-7:]
    nt = w_ref.shape[0]
    n = nt * LANES
    r, _ = row_factor(False, got_ref, None, w_ref, factor_ref, nt)
    put_rows(r_rows, r)
    fan, per = segments[0].shape[1:3]
    wide = fan * per // LANES
    blocks = nt // wide
    rt[...] = r.reshape(blocks, wide, LANES)
    slot = slot_of(me_ref[0], size)
    mine, home = slot & (fan - 1), slot // fan

    def weigh(i, _):
        block = load_block(segments, i, mine)
        b = i ^ home
        cols = jnp.concatenate([rt[b], jnp.zeros((8 - wide % 8, LANES), jnp.float32)], axis=0).T
        for t in range(wide):
            scaled = block[t * LANES : (t + 1) * LANES, :].astype(jnp.float32) * cols[:, t : t + 1]
            weighted[pl.ds(pl.multiple_of((b * wide + t) * LANES, LANES), LANES), :] = scaled.astype(jnp.bfloat16)
        return 0

    if len(segments) == blocks:
        for i in range(blocks):
            weigh(i, 0)
    else:
        lax.fori_loop(0, blocks, weigh, 0)
    kl = x_ref.shape[0]
    copies = []
    for i, k in enumerate(range(0, kl, kb)):
        x = x_ref[k : k + kb, :]
        col = col_ref[:, k : k + kb]
        mass = col * column_sums(x_ref, r_rows, k, kb) / balance
        load_ref[:, k : k + kb] = mass
        both = jnp.concatenate([mass, col / balance, jnp.zeros((6, kb), jnp.float32)], axis=0).T
        sums = jnp.dot(x, weighted[...], preferred_element_type=jnp.float32)
        stage[k : k + kb, :] = both[:, 0:1] * book_ref[k : k + kb, :].astype(jnp.float32) - both[:, 1:2] * sums
        copy = pltpu.make_async_copy(stage.at[k : k + kb, :], grad_ref.at[k : k + kb, :], sems.at[i])
        copy.start()
        copies.append(copy)
    for copy in copies:
        copy.wait()


def join_body(me_ref, own_ref, other_ref, out_ref, *, nt):
    wide = own_ref.shape[0] - nt
    copies = out_ref.shape[0]
    a, b = own_ref[:nt, :], other_ref[:nt, :]
    top = jnp.maximum(a, b)
    joined = top + jnp.log(jnp.exp(a - top) + jnp.exp(b - top))
    out_ref[:, :nt, :] = jnp.broadcast_to(joined[None], (copies, nt, LANES))
    odd = (me_ref[0] & 1) == 1
    a, b = own_ref[nt:, :], other_ref[nt:, :]
    out_ref[:, nt : nt + wide, :] = jnp.broadcast_to(jnp.where(odd, b, a)[None], (copies, wide, LANES))
    out_ref[:, nt + wide :, :] = jnp.broadcast_to(jnp.where(odd, a, b)[None], (copies, wide, LANES))


def share_first(lse, weights, me1, size, copies, nt):
    shard = weights.shape[0]
    code = lax.axis_size("code")
    groups = bit_groups(size)
    fan = 1 << len(groups[0])
    if copies == 1:
        lse = lse[:nt]
        top = lax.pmax(lse, AXES)
        common = top + jnp.log(lax.psum(jnp.exp(lse - top), AXES))
        w = lax.all_gather(weights, "rows", axis=0, tiled=True).reshape(size, shard // code)
        order = np.argsort([slot_int(g, size) for g in range(size)])
        return common[None], w[order].reshape(nt, LANES), None
    other = exchange(lse, 1, size)
    wide = lse.shape[0] - nt
    (message,) = call(
        functools.partial(join_body, nt=nt),
        "join",
        (me1, lse, other),
        [jax.ShapeDtypeStruct((size // 2, nt + 2 * wide, LANES), jnp.float32)],
        [],
    )
    same = [[i for i in range(size) if i % 2 == c] for c in range(2)]
    got = lax.all_to_all(message, AXES, split_axis=0, concat_axis=0, tiled=True, axis_index_groups=same)
    plan = [[] for _ in range(size // fan)]
    for g in range(size):
        plan[slot_int(g, size) // fan].append((g // 2, g % 2))
    return got, None, plan


def slot_int(device, size):
    bits = [bit for group in bit_groups(size) for bit in group[::-1]]
    return sum(1 << i for i, bit in enumerate(bits) if device & bit)


def share(send):
    if send.shape[0] == 1:
        return lax.psum(send.astype(jnp.float32), AXES)
    return lax.all_to_all(send, AXES, split_axis=0, concat_axis=0, tiled=True)


def copies_of(size, nt):
    return size if size * nt * LANES <= 1 << 20 else 1


IN_VMEM = pl.BlockSpec(memory_space=pltpu.VMEM)
IN_SMEM = pl.BlockSpec(memory_space=pltpu.SMEM)


def call(body, name, args, outs, scratch, out_specs=None, aliases=None, cost=None):
    return pl.pallas_call(
        body,
        in_specs=[IN_SMEM if a.dtype == jnp.int32 else IN_VMEM for a in args],
        out_specs=out_specs or [IN_VMEM] * len(outs),
        out_shape=outs,
        scratch_shapes=scratch,
        input_output_aliases=aliases or {},
        cost_estimate=cost,
        compiler_params=pltpu.CompilerParams(vmem_limit_bytes=VMEM_LIMIT),
        name=name,
    )(*args)


def local(embedding_vectors, codebook, weights):
    rows, code = lax.axis_size("rows"), lax.axis_size("code")
    size = rows * code
    shard, d = embedding_vectors.shape
    kl = codebook.shape[0]
    n = rows * shard
    nt = n // LANES
    balance = n / (size * kl)
    copies = copies_of(size, nt)
    me = (lax.axis_index("rows") * code + lax.axis_index("code")).astype(jnp.int32)
    per = shard // code
    piece = lax.dynamic_slice_in_dim(embedding_vectors, lax.axis_index("code") * per, per, 0)
    me1 = me.reshape(1)
    vec = jax.ShapeDtypeStruct((nt, LANES), jnp.float32)
    outs = [pltpu.VMEM((kl, n), jnp.bfloat16), pltpu.VMEM((nt, LANES), jnp.float32)]
    outs.append(pltpu.VMEM((nt + shard // LANES, LANES), jnp.float32))
    block = per << len(bit_groups(size)[0])

    def exponents(state, chosen, part, through=0):
        state = tuple(pltpu.with_memory_space_constraint(a, pltpu.VMEM) for a in state)
        args = (me1, weights, book, *part) + state
        count = sum(p.shape[0] for p in part)
        aliases = {3 + i: 3 + i for i in range(through)}
        if state:
            aliases.update({len(args) - 3 + i: i for i in range(3)})
        out = call(
            functools.partial(exponent_body, size=size, code=code, first=not state, start=chosen, through=through, kb=min(256, kl)),
            "exponents",
            args,
            outs + [jax.ShapeDtypeStruct(p.shape, p.dtype) for p in part[:through]],
            [pltpu.VMEM((2, kl, block), jnp.float32)],
            cost=pl.CostEstimate(
                flops=2 * kl * d * block * count, transcendentals=kl * block * count, bytes_accessed=6 * kl * block * count
            ),
            aliases=aliases,
        )
        return tuple(out[:3]), out[3:]

    book = pltpu.with_memory_space_constraint(codebook, pltpu.VMEM)
    if size == 32:
        first = piece[None]
        a0 = jnp.concatenate([first] + [exchange(first, m, size) for m in (8, 16, 24)], axis=0)[None]
        a1 = exchange(a0, 1, size)
        x0, y0, d0 = (exchange(a0, m, size) for m in (2, 4, 6))
        state, _ = exponents((), [0, 4], [a0, a1])
        state, (x0, y0) = exponents(state, [1, 2], [x0, y0], 2)
        x1, y1 = exchange(x0, 1, size), exchange(y0, 1, size)
        state, (d0,) = exponents(state, [3], [d0], 1)
        d1 = exchange(d0, 1, size)
        state, _ = exponents(state, [5, 6], [x1, y1])
        state, _ = exponents(state, [7], [d1])
        segments = [a0, x0, y0, d0, a1, x1, y1, d1]
    else:
        segments = gather_blocks(piece, size)
        state, _ = exponents((), list(range(len(segments))), segments)
    x, peak, lse = state
    x = pltpu.with_memory_space_constraint(x, pltpu.VMEM)
    got, w, plan = share_first(lse, weights, me1, size, copies, nt)
    row_scales = pltpu.VMEM((16, n), jnp.bfloat16)
    kb = min(256, kl)
    scratch = [row_scales, pltpu.VMEM((16, n), jnp.float32)]
    messages = jax.ShapeDtypeStruct((copies, nt, LANES), jnp.bfloat16)
    columns = jax.ShapeDtypeStruct((1, kl), jnp.float32)
    body = functools.partial(iterate_body, balance=balance, kb=kb, plan=plan)
    col, send, factor, w = call(functools.partial(body, first=True), "iterate_first", (got, peak, x) + (() if w is None else (w,)), [columns, messages, vec, vec], scratch)
    got = share(send)
    for _ in range(ITERS - 1):
        col, send = call(functools.partial(body, first=False), "iterate", (got, factor, w, x), [columns, messages], scratch)
        got = share(send)
    grad, load = call(
        functools.partial(final_body, size=size, balance=balance, kb=kb),
        "finish",
        (me1, got, factor, w, x, col, codebook, *segments),
        [jax.ShapeDtypeStruct((kl, d), jnp.float32), columns],
        [
            row_scales,
            pltpu.VMEM((n, d), jnp.bfloat16),
            pltpu.VMEM((n // block, block // LANES, LANES), jnp.float32),
            pltpu.VMEM((kl, d), jnp.float32),
            pltpu.SemaphoreType.DMA((kl // kb,)),
        ],
        [pl.BlockSpec(memory_space=pl.ANY), IN_VMEM],
    )
    return grad, load.reshape(kl)


def solution(mesh):
    placed = (P("rows", None), P(("code", "rows"), None), P("rows"))
    return jax.shard_map(
        local,
        mesh=mesh,
        in_specs=placed,
        out_specs=(P(("code", "rows"), None), P(("code", "rows"))),
        check_vma=False,
    )
```
